512 devices in a mesh: dp: 4 (over y), ep: 128 (over z, x, core).
Axes of the slice: x: 4, y: 4, z: 16, core: 2. Of those that a mesh axis runs over, the one named last changes fastest.
Arguments:
- tokens: bfloat16 [4096, 3584], P(('dp', 'ep')), may hold values from -6 to 6
- expert_ids: int32 [4096, 8], P(('dp', 'ep')), may hold values from 0 to 127, as said below
- route_gates: float32 [4096, 8], P(('dp', 'ep')), may hold values from 0.1 to 1
- w_gate: bfloat16 [128, 3584, 1024], P('ep', None, 'dp'), may hold values from -0.09375 to 0.09375
- w_up: bfloat16 [128, 3584, 1024], P('ep', None, 'dp'), may hold values from -0.09375 to 0.09375
Outputs:
- activations: bfloat16 [4096, 8, 1024], P(('dp', 'ep'))
The draws below stay inside these ranges and needn't reach their ends.
Inputs may be any that keep to these rules, and one draw needn't show every extreme that they name: `expert_ids`: each row names 8 different experts. Exactly 1 expert, the hot ones, are named by 8 tokens of every device each, and every token names exactly one of them. Any other expert is named by at most 2 tokens of one device, and some such expert is named by exactly 2 tokens of every device.
All inputs are finite; a program needn't handle non-finite values.
Results may differ from the reference program's by a relative error of at most 0.0049.
Values may be sent and summed in bfloat16 or wider, within the bound.
No kernel may reach another device: no remote copies, remote signals or barrier semaphores. Data moves between devices by JAX's collectives and lax.ppermute only.
A program may use at most 128 MiB of HBM per device.

```python
import jax
import jax.numpy as jnp
from jax import lax

D = 3584
FF = 1024
TOPK = 8
HOT = 1
TOK_DEV = 8
EXPERTS = 128
CAPC = 2
TOKENS = 4096


def draw_expert_ids(key, part):
    blocks = TOKENS // TOK_DEV
    cold_total = EXPERTS - HOT
    pick_total = (TOPK - 1) * TOK_DEV
    run_total = (pick_total + CAPC - 1) // CAPC
    reach = max(1, run_total // 2)
    shuffled = jax.random.permutation(jax.random.fold_in(key, 11), EXPERTS).astype(jnp.int32)
    hot_set = shuffled[:HOT]
    cold_set = shuffled[HOT:]
    shifts = jax.random.randint(jax.random.fold_in(key, 12), (blocks, 1, 1), 0, reach, dtype=jnp.int32)
    offsets = jax.random.randint(jax.random.fold_in(key, 13), (blocks, 1), 0, HOT, dtype=jnp.int32)
    turns = jax.random.randint(jax.random.fold_in(key, 14), (blocks, TOK_DEV, 1), 0, TOPK, dtype=jnp.int32)
    positions = jnp.arange(TOK_DEV, dtype=jnp.int32)
    tickets = positions[:, None] + TOK_DEV * jnp.arange(TOPK - 1, dtype=jnp.int32)[None, :]
    cold_pick = jnp.take(cold_set, (tickets[None, :, :] // CAPC + shifts) % cold_total)
    hot_pick = jnp.take(hot_set, (positions[None, :] + offsets) % HOT)
    rows_all = jnp.concatenate([hot_pick[:, :, None], cold_pick], axis=2)
    columns = (jnp.arange(TOPK, dtype=jnp.int32)[None, None, :] + turns) % TOPK
    return jnp.take_along_axis(rows_all, columns, axis=2).reshape(TOKENS, TOPK).astype(jnp.int32)


def shard_levels(stream_key, shape, cuts, low, top_value):
    loudness = 1.0
    for axis_at, shards_of in cuts:
        heights = jax.random.uniform(jax.random.fold_in(jax.random.fold_in(stream_key, 6), axis_at), (shards_of,), jnp.float32, low / len(cuts), top_value / len(cuts))
        loudness = loudness * jnp.repeat(jnp.exp(heights), shape[axis_at] // shards_of).reshape((-1,) + (1,) * (len(shape) - 1 - axis_at))
    return loudness


def bell_draw(own_key, shape, width, bound, cuts=(), kind=jnp.bfloat16):
    entries = width * jax.random.normal(own_key, shape, jnp.float32)
    if cuts:
        entries = entries * shard_levels(own_key, shape, cuts, -0.22, 0.18)
    return jnp.clip(entries, -bound, bound).astype(kind)


def setup_inputs(seed: int = 0) -> dict:
    splits = jax.random.split(jax.random.key(seed), 6)
    tokens = bell_draw(splits[0], (TOKENS, D), 1.0, 6.0, ((0, 512),))
    expert_ids = draw_expert_ids(jax.random.fold_in(splits[5], 71), 0)
    route_gates = jnp.clip(0.1 + 0.9 * jax.random.uniform(splits[2], (TOKENS, TOPK), jnp.float32) ** shard_levels(splits[2], (TOKENS, TOPK), ((0, 512),), -0.2, 0.2), 0.1, 1.0)
    w_gate = bell_draw(splits[3], (EXPERTS, D, FF), D ** -0.5, 0.09375, ((0, 128), (2, 4)))
    w_up = bell_draw(splits[4], (EXPERTS, D, FF), D ** -0.5, 0.09375, ((0, 128), (2, 4)))
    return dict(tokens=tokens, expert_ids=expert_ids, route_gates=route_gates, w_gate=w_gate, w_up=w_up)


def block_slots(block_ids, cold_mask):
    labels = jnp.arange(EXPERTS, dtype=jnp.int32)
    matches = jnp.logical_and(block_ids[:, None] == labels[None, :], cold_mask[:, None]).astype(jnp.int32)
    before = jnp.cumsum(matches, axis=0) - matches
    return jnp.sum(before * matches, axis=1).astype(jnp.int32)


def gated(row_block, gate_cols, up_cols):
    gate_part = jnp.dot(row_block, gate_cols, preferred_element_type=jnp.float32)
    up_part = jnp.dot(row_block, up_cols, preferred_element_type=jnp.float32)
    return (jax.nn.silu(gate_part) * up_part).astype(jnp.bfloat16)


def reference(tokens, expert_ids, route_gates, w_gate, w_up):
    blocks = TOKENS // TOK_DEV
    labels = jnp.arange(EXPERTS, dtype=jnp.int32)
    counts = jnp.zeros((EXPERTS,), jnp.int32).at[expert_ids.reshape(-1)].add(1)
    scores = counts * EXPERTS + (EXPERTS - 1 - labels)
    hot_ids = lax.top_k(scores, HOT)[1].astype(jnp.int32)
    rank_of = jnp.full((EXPERTS,), HOT, jnp.int32).at[hot_ids].set(jnp.arange(HOT, dtype=jnp.int32))
    pick_rank = rank_of[expert_ids]
    is_hot = pick_rank < HOT
    slots = lax.map(lambda inputs: block_slots(inputs[0], inputs[1]), (expert_ids.reshape(blocks, TOK_DEV * TOPK), jnp.logical_not(is_hot).reshape(blocks, TOK_DEV * TOPK))).reshape(TOKENS, TOPK)
    token_of = jnp.broadcast_to(jnp.arange(TOKENS, dtype=jnp.int32)[:, None], (TOKENS, TOPK))
    block_of = (token_of // TOK_DEV).astype(jnp.int32)
    column = (block_of * CAPC + slots).astype(jnp.int32)
    target = jnp.where(is_hot, EXPERTS, expert_ids).astype(jnp.int32)
    table = jnp.zeros((EXPERTS, blocks * CAPC), jnp.int32).at[target, column].set(token_of, mode="drop")

    def serve(inputs):
        row_index, gate_cols, up_cols = inputs
        return gated(jnp.take(tokens, row_index, axis=0), gate_cols, up_cols)

    cold_hidden = lax.map(serve, (table, w_gate, w_up))
    hot_hidden = lax.map(lambda expert: gated(tokens, w_gate[expert], w_up[expert]), hot_ids)
    picked_cold = cold_hidden[jnp.where(is_hot, 0, expert_ids).astype(jnp.int32), jnp.where(is_hot, 0, column).astype(jnp.int32)]
    picked_hot = hot_hidden[jnp.minimum(pick_rank, HOT - 1).astype(jnp.int32), token_of]
    picked = jnp.where(is_hot[:, :, None], picked_hot, picked_cold)
    return (route_gates[:, :, None] * picked.astype(jnp.float32)).astype(jnp.bfloat16)
```

```python
import jax
import jax.numpy as jnp
from jax import lax
from jax.sharding import Mesh, PartitionSpec as P

EP_AXES = ("z", "x", "core")
ALL_AXES = ("dp",) + EP_AXES


def per_device(tokens, expert_ids, route_gates, w_gate, w_up):
    tok_rows, top_count = expert_ids.shape
    quarter = w_gate.shape[2]
    groups = lax.axis_size("dp")
    owners = lax.axis_size(EP_AXES)
    column = lax.all_gather(tokens, "z", axis=0, tiled=True)
    everyone = lax.all_gather(column, ("dp", "x", "core"), axis=0, tiled=True)
    gate_part = jnp.dot(everyone, w_gate[0], preferred_element_type=jnp.float32)
    up_part = jnp.dot(everyone, w_up[0], preferred_element_type=jnp.float32)
    hidden = (jax.nn.silu(gate_part) * up_part).astype(jnp.bfloat16)
    depth, width, cores = (lax.axis_size(a) for a in EP_AXES)
    blocks = hidden.reshape(groups, width * cores, depth, tok_rows, quarter)
    blocks = blocks.swapaxes(1, 2).reshape(groups * owners, tok_rows, quarter)
    home = lax.all_to_all(blocks, ALL_AXES, split_axis=0, concat_axis=0, tiled=True)
    table = home.reshape(groups * owners * tok_rows, quarter)
    rows = expert_ids * tok_rows + jnp.arange(tok_rows, dtype=jnp.int32)[:, None]
    starts = jnp.arange(groups, dtype=jnp.int32) * (owners * tok_rows)
    rows = starts[:, None] + rows.reshape(-1)[None, :]
    picked = jnp.take(table, rows.reshape(-1), axis=0).reshape(
        groups, tok_rows, top_count, quarter
    )
    hidden = picked.transpose(1, 2, 0, 3).reshape(tok_rows, top_count, groups * quarter)
    return (route_gates[:, :, None] * hidden.astype(jnp.float32)).astype(jnp.bfloat16)


def solution(mesh):
    depth, width, cores = 16, 4, 2
    groups = mesh.shape["dp"]
    fine = Mesh(mesh.devices.reshape(groups, depth, width, cores), ALL_AXES)
    return jax.shard_map(
        per_device,
        mesh=fine,
        in_specs=(
            P(ALL_AXES, None),
            P(ALL_AXES, None),
            P(ALL_AXES, None),
            P(EP_AXES, None, "dp"),
            P(EP_AXES, None, "dp"),
        ),
        out_specs=P(ALL_AXES, None, None),
        check_vma=False,
    )
```

```python
import functools

import jax
import jax.numpy as jnp
from jax import lax
from jax.experimental import pallas as pl
from jax.experimental.pallas import tpu as pltpu
from jax.sharding import Mesh, PartitionSpec as P

EP_AXES = ("z", "x", "core")
ALL_AXES = ("dp",) + EP_AXES
FLOW_AXES = ("dp", "x", "core", "z")
SLOTS = 2
LANES = 128
COLUMNS_PER_STEP = 4
F32 = jnp.float32
BF16 = jnp.bfloat16


def expert_kernel(own_ref, hot_ref, rows_ref, gate_ref, up_ref, cold_ref, hot_out_ref, *, tok_rows):
    width = gate_ref.shape[0]
    block = rows_ref.shape[0]
    homes = block // tok_rows
    rows = rows_ref[:, :width]
    gate_part = jnp.dot(rows, gate_ref[...], preferred_element_type=F32)
    up_part = jnp.dot(rows, up_ref[...], preferred_element_type=F32)
    hidden = (gate_part / (1.0 + jnp.exp(-gate_part)) * up_part).astype(BF16)
    wide = hidden.astype(F32)
    mine = jnp.where(hot_ref[0] > 0, wide, 0.0).astype(BF16)
    hot_out_ref[...] = mine.reshape(hot_out_ref.shape)

    ids = rows_ref[:, width:].astype(F32)
    hits = jnp.where(ids == own_ref[0].astype(F32), 1.0, 0.0).astype(BF16)
    named = jnp.dot(hits, jnp.ones((LANES, LANES), BF16), preferred_element_type=F32)
    row_at = lax.broadcasted_iota(jnp.int32, (block, block), 0)
    col_at = lax.broadcasted_iota(jnp.int32, (block, block), 1)
    earlier = jnp.logical_and(row_at // tok_rows == col_at // tok_rows, col_at < row_at)
    before = jnp.dot(
        jnp.where(earlier, 1.0, 0.0).astype(BF16), named.astype(BF16), preferred_element_type=F32
    )
    home_at = lax.broadcasted_iota(jnp.int32, (homes, block), 0)
    from_at = lax.broadcasted_iota(jnp.int32, (homes, block), 1)
    of_home = jnp.where(from_at // tok_rows == home_at, 1.0, 0.0).astype(BF16)
    quarter = hidden.shape[1]
    for slot in range(SLOTS):
        chosen = jnp.where(before == float(slot), named, 0.0)
        chosen = jnp.concatenate([chosen] * (quarter // LANES), axis=1)
        kept = (wide * chosen).astype(BF16)
        cold_ref[:, slot * quarter : (slot + 1) * quarter] = jnp.dot(
            of_home, kept, preferred_element_type=F32
        ).astype(BF16)


def home_kernel(place_ref, gate_ref, cold_ref, hot_ref, out_ref, *, groups, tok_rows):
    pairs = out_ref.shape[0]
    quarter = hot_ref.shape[2]
    owners = cold_ref.shape[0] // groups
    place = place_ref[...]
    lane_at = lax.broadcasted_iota(jnp.int32, (pairs, owners), 1)
    picks = [
        jnp.where(place == lane_at * SLOTS + slot, 1.0, 0.0).astype(BF16) for slot in range(SLOTS)
    ]
    tok_at = lax.broadcasted_iota(jnp.int32, (pairs, tok_rows), 0) // (pairs // tok_rows)
    row_at = lax.broadcasted_iota(jnp.int32, (pairs, tok_rows), 1)
    hot_pick = jnp.where(jnp.logical_and(place < 0, tok_at == row_at), 1.0, 0.0).astype(BF16)
    gates = gate_ref[...]
    for group in range(groups):
        total = jnp.dot(hot_pick, hot_ref[group], preferred_element_type=F32)
        for slot in range(SLOTS):
            total += jnp.dot(
                picks[slot],
                cold_ref[group * owners : (group + 1) * owners, slot * quarter : (slot + 1) * quarter],
                preferred_element_type=F32,
            )
        out_ref[:, group * quarter : (group + 1) * quarter] = (gates * total).astype(BF16)


def per_device(tokens, expert_ids, route_gates, w_gate, w_up):
    tok_rows, top_count = expert_ids.shape
    model_width = tokens.shape[1]
    quarter = w_gate.shape[2]
    groups = lax.axis_size("dp")
    depth, width, cores = (lax.axis_size(a) for a in EP_AXES)
    columns = width * cores
    owners = depth * columns
    total = groups * owners
    own = lax.axis_index(EP_AXES).astype(jnp.int32)

    id_part = jnp.pad(
        expert_ids.astype(BF16), ((0, 0), (0, LANES - top_count)), constant_values=-1
    )
    packed = jnp.concatenate([tokens, id_part], axis=1)
    line = lax.all_gather(packed, "z", axis=0, tiled=True)
    expert_ids, line = lax.optimization_barrier((expert_ids, line))
    everyone = lax.all_gather(line, ("dp", "x", "core"), axis=0, tiled=True)

    named_by = jnp.any(
        expert_ids[:, :, None, None] == expert_ids[None, None, :, :], axis=3
    ).astype(jnp.int32)
    is_hot = jnp.sum(named_by, axis=2) > SLOTS
    is_before = (
        jnp.arange(tok_rows)[None, None, :] < jnp.arange(tok_rows)[:, None, None]
    ).astype(jnp.int32)
    slots = jnp.sum(named_by * is_before, axis=2)
    hot_id = jnp.max(jnp.where(is_hot, expert_ids, -1))
    at_z = expert_ids // columns
    at_column = expert_ids % columns
    place = (at_column * depth + at_z) * SLOTS + slots
    place = jnp.where(is_hot, -1, place).reshape(tok_rows * top_count, 1)

    column_rows = depth * tok_rows
    per_step = COLUMNS_PER_STEP
    steps = columns // per_step
    block = per_step * column_rows
    cold, hot = pl.pallas_call(
        functools.partial(expert_kernel, tok_rows=tok_rows),
        grid=(groups * steps,),
        out_shape=(
            jax.ShapeDtypeStruct((total, SLOTS * quarter), BF16),
            jax.ShapeDtypeStruct((columns, groups, column_rows, quarter), BF16),
        ),
        in_specs=[
            pl.BlockSpec(memory_space=pltpu.SMEM),
            pl.BlockSpec(memory_space=pltpu.SMEM),
            pl.BlockSpec((block, model_width + LANES), lambda i: (i, 0)),
            pl.BlockSpec((model_width, quarter), lambda i: (0, 0)),
            pl.BlockSpec((model_width, quarter), lambda i: (0, 0)),
        ],
        out_specs=(
            pl.BlockSpec((block // tok_rows, SLOTS * quarter), lambda i: (i, 0)),
            pl.BlockSpec(
                (per_step, 1, column_rows, quarter), lambda i: (i % steps, i // steps, 0, 0)
            ),
        ),
        compiler_params=pltpu.CompilerParams(vmem_limit_bytes=48 * 2**20),
        name="expert",
    )(
        own.reshape(1),
        (own == hot_id).astype(jnp.int32).reshape(1),
        everyone,
        w_gate.reshape(model_width, quarter),
        w_up.reshape(model_width, quarter),
    )

    hot = lax.psum_scatter(
        hot.reshape(columns * groups * column_rows, quarter),
        ("x", "core"),
        scatter_dimension=0,
        tiled=True,
    )
    cold = lax.all_to_all(
        cold.reshape(total, SLOTS, quarter), FLOW_AXES, split_axis=0, concat_axis=0, tiled=True
    )
    hot = lax.all_to_all(
        hot.reshape(groups * depth, tok_rows, quarter),
        ("dp", "z"),
        split_axis=0,
        concat_axis=0,
        tiled=True,
    )
    hot = lax.dynamic_index_in_dim(
        hot.reshape(groups, depth, tok_rows, quarter), hot_id // columns, 1, keepdims=False
    )
    pairs = tok_rows * top_count
    out = pl.pallas_call(
        functools.partial(home_kernel, groups=groups, tok_rows=tok_rows),
        out_shape=jax.ShapeDtypeStruct((pairs, groups * quarter), BF16),
        name="home",
    )(place, route_gates.reshape(pairs, 1), cold.reshape(total, SLOTS * quarter), hot)
    return out.reshape(tok_rows, top_count, groups * quarter)


def solution(mesh):
    width, cores = 4, 2
    groups, depth = mesh.shape["dp"], mesh.shape["ep"] // (width * cores)
    fine = Mesh(mesh.devices.reshape(groups, depth, width, cores), ALL_AXES)
    return jax.shard_map(
        per_device,
        mesh=fine,
        in_specs=(
            P(ALL_AXES, None),
            P(ALL_AXES, None),
            P(ALL_AXES, None),
            P(EP_AXES, None, "dp"),
            P(EP_AXES, None, "dp"),
        ),
        out_specs=P(ALL_AXES, None, None),
        check_vma=False,
    )
```

```python
import functools

import jax
import jax.numpy as jnp
from jax import lax
from jax.experimental import pallas as pl
from jax.experimental.pallas import tpu as pltpu
from jax.sharding import Mesh, PartitionSpec as P

EP_AXES = ("z", "x", "core")
ALL_AXES = ("dp",) + EP_AXES
SLOTS = 2
LANES = 128
CORES = 2
RING = 4
OFFSETS = (0, -1, 1, 2)
F32 = jnp.float32
BF16 = jnp.bfloat16


def expert_kernel(
    scalar_ref, low_ref, high_ref, gate0, up0, gate1, up1, *rest, tok_rows, aliased
):
    out_ref, hidden_ref, ids_ref, pay_ref = rest[1:] if aliased else rest
    width, quarter = gate0.shape
    block = low_ref.shape[0] + high_ref.shape[0]
    homes = block // tok_rows
    step = pl.program_id(0)

    @pl.when(step == 0)
    def _():
        rows = jnp.concatenate([low_ref[:, :width], high_ref[:, :width]], axis=0)
        half = low_ref.shape[0]
        ids_ref[:half, :] = low_ref[:, width:].astype(F32)
        ids_ref[half:, :] = high_ref[:, width:].astype(F32)
        for place, (gate, up) in enumerate(((gate0, up0), (gate1, up1))):
            gate_part = jnp.dot(rows, gate[...], preferred_element_type=F32)
            up_part = jnp.dot(rows, up[...], preferred_element_type=F32)
            hidden = (gate_part / (1.0 + jnp.exp(-gate_part)) * up_part).astype(BF16)
            for part in range(quarter // LANES):
                hidden_ref[place, part] = hidden[:, part * LANES : (part + 1) * LANES].astype(F32)

        def rows_at(place, tok):
            every = pl.ds(tok, homes, stride=tok_rows)
            parts = [hidden_ref[place, part, every, :] for part in range(quarter // LANES)]
            return jnp.concatenate(parts, axis=1)

        for place in range(CORES):
            expert = scalar_ref[RING * RING + place].astype(F32)
            count = jnp.zeros((homes, 1), F32)
            totals = [jnp.zeros((homes, quarter), F32) for _ in range(SLOTS)]
            for tok in range(tok_rows):
                every = pl.ds(tok, homes, stride=tok_rows)
                value = rows_at(place, tok)
                named = jnp.max(
                    jnp.where(ids_ref[every, :] == expert, 1.0, 0.0), axis=1, keepdims=True
                )
                for slot in range(SLOTS):
                    take = jnp.where(count == float(slot), named, 0.0)
                    totals[slot] = totals[slot] + take * value
                count = count + named
            for slot in range(SLOTS):
                at = (place * SLOTS + slot) * quarter
                pay_ref[:, at : at + quarter] = totals[slot].astype(BF16)
        for tok in range(tok_rows):
            value = jnp.where(scalar_ref[RING * RING + CORES] > 0, rows_at(0, tok), 0.0)
            value += jnp.where(scalar_ref[RING * RING + CORES + 1] > 0, rows_at(1, tok), 0.0)
            at = (CORES * SLOTS + tok) * quarter
            pay_ref[:, at : at + quarter] = value.astype(BF16)

    rows_out = out_ref.shape[1]
    out_ref[0] = pay_ref[pl.ds(pl.multiple_of(step * rows_out, rows_out), rows_out), :]


def serve(scalars, number, low, high, weights, so_far, tok_rows, depth):
    quarter = weights[0].shape[1]
    block = low.shape[0] + high.shape[0]
    lanes = (CORES * SLOTS + tok_rows) * quarter
    whole = lambda a: pl.BlockSpec(a.shape, lambda i, s: (0, 0))
    operands = [low, high, *weights]
    in_specs = [whole(a) for a in operands]
    aliases = {}
    if so_far is not None:
        aliases = {1 + len(operands): 0}
        operands.append(so_far)
        in_specs.append(pl.BlockSpec(memory_space=pl.ANY))
    return pl.pallas_call(
        functools.partial(expert_kernel, tok_rows=tok_rows, aliased=so_far is not None),
        grid_spec=pltpu.PrefetchScalarGridSpec(
            num_scalar_prefetch=1,
            grid=(RING,),
            in_specs=in_specs,
            out_specs=pl.BlockSpec((1, depth, lanes), lambda i, s: (s[RING * number + i], 0, 0)),
            scratch_shapes=[
                pltpu.VMEM((CORES, quarter // LANES, block, LANES), F32),
                pltpu.VMEM((block, LANES), F32),
                pltpu.VMEM((block // tok_rows, lanes), BF16),
            ],
        ),
        out_shape=jax.ShapeDtypeStruct((RING * RING, depth, lanes), BF16),
        input_output_aliases=aliases,
        compiler_params=pltpu.CompilerParams(vmem_limit_bytes=48 * 2**20),
        cost_estimate=pl.CostEstimate(
            flops=2 * block * weights[0].shape[0] * quarter * 4,
            bytes_accessed=2 * (block * low.shape[1] + 4 * weights[0].size + RING * depth * lanes),
            transcendentals=2 * block * quarter,
        ),
        name="expert",
    )(scalars, *operands)


def assemble_kernel(hot_x_ref, near_ref, out_ref, wide_ref, *, tok_rows):
    width, homes, _ = near_ref.shape
    count = out_ref.shape[0] // homes
    quarter = out_ref.shape[1]
    parts = quarter // LANES
    for row in range(count):
        if row < count - tok_rows:
            source, entry = divmod(row, CORES * SLOTS)
        else:
            source, entry = hot_x_ref[0], row - (count - tok_rows) + CORES * SLOTS
        for part in range(parts):
            at = entry * quarter + part * LANES
            wide_ref[part, pl.ds(row, homes, stride=count), :] = near_ref[
                source, :, at : at + LANES
            ].astype(F32)
    for part in range(parts):
        out_ref[:, part * LANES : (part + 1) * LANES] = wide_ref[part].astype(BF16)


def home_kernel(place_ref, gate_ref, rows_ref, out_ref):
    pairs = out_ref.shape[0]
    groups, count, quarter = rows_ref.shape
    row_at = lax.broadcasted_iota(jnp.int32, (pairs, count), 1)
    pick = jnp.where(place_ref[...] == row_at, 1.0, 0.0).astype(BF16)
    gates = gate_ref[...]
    for group in range(groups):
        value = jnp.dot(pick, rows_ref[group], preferred_element_type=F32)
        out_ref[:, group * quarter : (group + 1) * quarter] = (gates * value).astype(BF16)


def per_device(tokens, expert_ids, route_gates, w_gate, w_up, *, sizes):
    tok_rows, top_count = expert_ids.shape
    model_width = tokens.shape[1]
    quarter = w_gate.shape[2]
    groups, depth, width, cores = sizes
    columns = width * cores
    at_y, at_z, at_x, at_core = (lax.axis_index(a).astype(jnp.int32) for a in ALL_AXES)
    own = (at_z * width + at_x) * cores + at_core
    partner = own + 1 - 2 * at_core

    def linear(y, z, x, core):
        return ((y % groups * depth + z) * width + x % width) * cores + core

    def shift(value, first, by):
        pairs = []
        for y in range(groups):
            for z in range(depth):
                for x in range(width):
                    for core in range(cores):
                        along_y = (core == 0) == first
                        to = (y + by, z, x, core) if along_y else (y, z, x + by, core)
                        pairs.append((linear(y, z, x, core), linear(*to)))
        return lax.ppermute(value, ALL_AXES, pairs)

    id_part = jnp.pad(
        expert_ids.astype(BF16), ((0, 0), (0, LANES - top_count)), constant_values=-1
    )
    line = lax.all_gather(
        jnp.concatenate([tokens, id_part], axis=1), "z", axis=0, tiled=True
    )
    expert_ids, w_gate, w_up, line = lax.optimization_barrier((expert_ids, w_gate, w_up, line))

    before = shift(line, True, 1)
    after = shift(line, True, -1)
    mine = (w_gate.reshape(model_width, quarter), w_up.reshape(model_width, quarter))
    swap = [(0, 1), (1, 0)]
    weights = mine + tuple(lax.ppermute(a, "core", swap) for a in mine)
    low = jnp.concatenate([line, before], axis=0)
    low_before = shift(low, False, 1)
    low_after = shift(low, False, -1)
    half = line.shape[0] // 2
    far = [shift(before[:half], True, 1), shift(after[half:], True, -1)]
    high = jnp.concatenate([after] + far, axis=0)
    high_before = shift(high, False, 1)
    high_after = shift(high, False, -1)
    low_far = shift(low_before, False, 1)
    high_far = shift(high_after, False, -1)

    named_by = jnp.any(
        expert_ids[:, :, None, None] == expert_ids[None, None, :, :], axis=3
    ).astype(jnp.int32)
    is_hot = jnp.sum(named_by, axis=2) > SLOTS
    tok_at = jnp.arange(tok_rows, dtype=jnp.int32)
    is_before = (tok_at[None, None, :] < tok_at[:, None, None]).astype(jnp.int32)
    slots = jnp.sum(named_by * is_before, axis=2)
    hot_id = jnp.max(jnp.where(is_hot, expert_ids, -1))
    cold_rows = columns * SLOTS
    rows = cold_rows + tok_rows
    place = expert_ids % columns // cores * (cores * SLOTS)
    place = place + jnp.bitwise_xor(expert_ids % cores, at_core) * SLOTS + slots
    place = jnp.where(is_hot, cold_rows + tok_at[:, None], place)
    place = (place + expert_ids // columns * rows).reshape(tok_rows * top_count, 1)

    lane_at = jnp.arange(2 * RING * RING, dtype=jnp.int32)
    offset_of = lambda at: jnp.where(at == 3, 2, jnp.where(at == 2, 1, -at))
    first = offset_of(lane_at % RING)
    second = offset_of(lane_at // RING % RING)
    y_to = (at_y + jnp.where(at_core == 0, first, second)) % groups
    x_to = (at_x + jnp.where(at_core == 0, second, first)) % width
    served_id = jnp.where(lane_at % CORES == 0, own, partner)
    flag = jnp.where(lane_at % RING < CORES, served_id, (served_id == hot_id).astype(jnp.int32))
    scalars = jnp.where(lane_at < RING * RING, x_to * groups + y_to, flag)

    served = None
    pieces = ((low, high), (low_before, high_before), (low_after, high_after), (low_far, high_far))
    for number, piece in enumerate(pieces):
        served = serve(scalars, number, *piece, weights, served, tok_rows, depth)

    lanes = served.shape[2]
    homes = groups * depth
    near = lax.all_to_all(
        served.reshape(width, homes, lanes), "x", split_axis=0, concat_axis=0, tiled=True
    )
    send = pl.pallas_call(
        functools.partial(assemble_kernel, tok_rows=tok_rows),
        in_specs=[
            pl.BlockSpec(memory_space=pltpu.SMEM),
            pl.BlockSpec(memory_space=pltpu.VMEM),
        ],
        out_shape=jax.ShapeDtypeStruct((homes * rows, quarter), BF16),
        scratch_shapes=[pltpu.VMEM((quarter // LANES, homes * rows, LANES), F32)],
        name="assemble",
    )((hot_id % columns // cores).reshape(1), near).reshape(homes, rows, quarter)
    back = lax.all_to_all(send, ("dp", "z"), split_axis=0, concat_axis=0, tiled=True)
    pairs = tok_rows * top_count
    out = pl.pallas_call(
        home_kernel,
        out_shape=jax.ShapeDtypeStruct((pairs, groups * quarter), BF16),
        name="home",
    )(place, route_gates.reshape(pairs, 1), back.reshape(groups, depth * rows, quarter))
    return out.reshape(tok_rows, top_count, groups * quarter)


def solution(mesh):
    groups = mesh.shape["dp"]
    sizes = (groups, mesh.shape["ep"] // (RING * CORES), RING, CORES)
    fine = Mesh(mesh.devices.reshape(sizes), ALL_AXES)
    return jax.shard_map(
        functools.partial(per_device, sizes=sizes),
        mesh=fine,
        in_specs=(
            P(ALL_AXES, None),
            P(ALL_AXES, None),
            P(ALL_AXES, None),
            P(EP_AXES, None, "dp"),
            P(EP_AXES, None, "dp"),
        ),
        out_specs=P(ALL_AXES, None, None),
        check_vma=False,
    )
```

```python
import functools

import jax
import jax.numpy as jnp
from jax import lax
from jax.experimental import pallas as pl
from jax.experimental.pallas import tpu as pltpu
from jax.sharding import Mesh, PartitionSpec as P


EP_AXES = ("z", "x", "core")
ALL_AXES = ("dp",) + EP_AXES
SLOTS = 2
LANES = 128
CORES = 2
RING = 4
F32 = jnp.float32
BF16 = jnp.bfloat16


def expert_kernel(
    scalar_ref, low_ref, high_ref, gate0, up0, gate1, up1, *rest, tok_rows, aliased
):
    refs = rest[1:] if aliased else rest
    out_ref, rows_ref, weight_ref, hidden_ref, ids_ref, pay_ref, sems = refs
    width, quarter = gate0.shape
    block = rows_ref.shape[0]
    homes = block // tok_rows
    step = pl.program_id(0)

    @pl.when(step == 0)
    def _():
        half = low_ref.shape[0]
        moves = [
            (low_ref, rows_ref.at[pl.ds(0, half)]),
            (high_ref, rows_ref.at[pl.ds(half, block - half)]),
        ]
        moves += [(ref, weight_ref.at[i]) for i, ref in enumerate((gate0, up0, gate1, up1))]
        copies = [pltpu.make_async_copy(a, b, sems.at[i]) for i, (a, b) in enumerate(moves)]
        for copy in copies:
            copy.start()
        copies[0].wait()
        copies[1].wait()
        rows = rows_ref[:, :width]
        ids_ref[...] = rows_ref[:, width:].astype(F32)
        for place in range(CORES):
            copies[2 + 2 * place].wait()
            gate_part = jnp.dot(rows, weight_ref[2 * place], preferred_element_type=F32)
            copies[3 + 2 * place].wait()
            up_part = jnp.dot(rows, weight_ref[2 * place + 1], preferred_element_type=F32)
            hidden = (gate_part / (1.0 + jnp.exp(-gate_part)) * up_part).astype(BF16)
            for part in range(quarter // LANES):
                hidden_ref[place, part] = hidden[:, part * LANES : (part + 1) * LANES].astype(F32)

        def rows_at(place, tok):
            every = pl.ds(tok, homes, stride=tok_rows)
            parts = [hidden_ref[place, part, every, :] for part in range(quarter // LANES)]
            return jnp.concatenate(parts, axis=1)

        for place in range(CORES):
            expert = scalar_ref[RING * RING + place].astype(F32)
            count = jnp.zeros((homes, 1), F32)
            totals = [jnp.zeros((homes, quarter), F32) for _ in range(SLOTS)]
            for tok in range(tok_rows):
                every = pl.ds(tok, homes, stride=tok_rows)
                value = rows_at(place, tok)
                named = jnp.max(
                    jnp.where(ids_ref[every, :] == expert, 1.0, 0.0), axis=1, keepdims=True
                )
                for slot in range(SLOTS):
                    take = jnp.where(count == float(slot), named, 0.0)
                    totals[slot] = totals[slot] + take * value
                count = count + named
            for slot in range(SLOTS):
                at = (place * SLOTS + slot) * quarter
                pay_ref[:, at : at + quarter] = totals[slot].astype(BF16)
        for tok in range(tok_rows):
            value = jnp.where(scalar_ref[RING * RING + CORES] > 0, rows_at(0, tok), 0.0)
            value += jnp.where(scalar_ref[RING * RING + CORES + 1] > 0, rows_at(1, tok), 0.0)
            at = (CORES * SLOTS + tok) * quarter
            pay_ref[:, at : at + quarter] = value.astype(BF16)

    rows_out = out_ref.shape[1]
    out_ref[0] = pay_ref[pl.ds(pl.multiple_of(step * rows_out, rows_out), rows_out), :]


def serve(scalars, number, low, high, weights, so_far, tok_rows, depth):
    quarter = weights[0].shape[1]
    block = low.shape[0] + high.shape[0]
    lanes = (CORES * SLOTS + tok_rows) * quarter
    operands = [low, high, *weights]
    in_specs = [pl.BlockSpec(memory_space=pl.ANY) for _ in operands]
    aliases = {}
    if so_far is not None:
        aliases = {1 + len(operands): 0}
        operands.append(so_far)
        in_specs.append(pl.BlockSpec(memory_space=pl.ANY))
    return pl.pallas_call(
        functools.partial(expert_kernel, tok_rows=tok_rows, aliased=so_far is not None),
        grid_spec=pltpu.PrefetchScalarGridSpec(
            num_scalar_prefetch=1,
            grid=(RING,),
            in_specs=in_specs,
            out_specs=pl.BlockSpec((1, depth, lanes), lambda i, s: (s[RING * number + i], 0, 0)),
            scratch_shapes=[
                pltpu.VMEM((block, low.shape[1]), BF16),
                pltpu.VMEM((2 * CORES,) + weights[0].shape, BF16),
                pltpu.VMEM((CORES, quarter // LANES, block, LANES), F32),
                pltpu.VMEM((block, LANES), F32),
                pltpu.VMEM((block // tok_rows, lanes), BF16),
                pltpu.SemaphoreType.DMA((2 + 2 * CORES,)),
            ],
        ),
        out_shape=jax.ShapeDtypeStruct((RING * RING, depth, lanes), BF16),
        input_output_aliases=aliases,
        compiler_params=pltpu.CompilerParams(vmem_limit_bytes=32 * 2**20),
        cost_estimate=pl.CostEstimate(
            flops=2 * block * weights[0].shape[0] * quarter * 4,
            bytes_accessed=2 * (block * low.shape[1] + 4 * weights[0].size + RING * depth * lanes),
            transcendentals=2 * block * quarter,
        ),
        name="expert",
    )(scalars, *operands)


def assemble_kernel(hot_x_ref, near_ref, out_ref, wide_ref, *, tok_rows):
    _, homes, _ = near_ref.shape
    count = out_ref.shape[0] // homes
    quarter = out_ref.shape[1]
    parts = quarter // LANES
    for row in range(count):
        if row < count - tok_rows:
            source, entry = divmod(row, CORES * SLOTS)
        else:
            source, entry = hot_x_ref[0], row - (count - tok_rows) + CORES * SLOTS
        for part in range(parts):
            at = entry * quarter + part * LANES
            wide_ref[part, pl.ds(row, homes, stride=count), :] = near_ref[
                source, :, at : at + LANES
            ].astype(F32)
    for part in range(parts):
        out_ref[:, part * LANES : (part + 1) * LANES] = wide_ref[part].astype(BF16)


def home_kernel(place_ref, gate_ref, rows_ref, out_ref):
    pairs = out_ref.shape[0]
    groups, count, quarter = rows_ref.shape
    row_at = lax.broadcasted_iota(jnp.int32, (pairs, count), 1)
    pick = jnp.where(place_ref[...] == row_at, 1.0, 0.0).astype(BF16)
    gates = gate_ref[...]
    for group in range(groups):
        value = jnp.dot(pick, rows_ref[group], preferred_element_type=F32)
        out_ref[:, group * quarter : (group + 1) * quarter] = (gates * value).astype(BF16)


def per_device(tokens, expert_ids, route_gates, w_gate, w_up, *, sizes):
    tok_rows, top_count = expert_ids.shape
    model_width = tokens.shape[1]
    quarter = w_gate.shape[2]
    groups, depth, width, cores = sizes
    columns = width * cores
    at_y, at_z, at_x, at_core = (lax.axis_index(a).astype(jnp.int32) for a in ALL_AXES)
    own = (at_z * width + at_x) * cores + at_core
    partner = own + 1 - 2 * at_core

    def linear(y, z, x, core):
        return ((y % groups * depth + z) * width + x % width) * cores + core

    def shift(value, first, by):
        pairs = []
        for y in range(groups):
            for z in range(depth):
                for x in range(width):
                    for core in range(cores):
                        along_y = (core == 0) == first
                        to = (y + by, z, x, core) if along_y else (y, z, x + by, core)
                        pairs.append((linear(y, z, x, core), linear(*to)))
        return lax.ppermute(value, ALL_AXES, pairs)

    id_part = jnp.pad(
        expert_ids.astype(BF16), ((0, 0), (0, LANES - top_count)), constant_values=-1
    )
    line = lax.all_gather(
        jnp.concatenate([tokens, id_part], axis=1), "z", axis=0, tiled=True
    )
    expert_ids, w_gate, w_up, line = lax.optimization_barrier((expert_ids, w_gate, w_up, line))

    before = shift(line, True, 1)
    after = shift(line, True, -1)
    mine = (w_gate.reshape(model_width, quarter), w_up.reshape(model_width, quarter))
    swap = [(0, 1), (1, 0)]
    theirs = (lax.ppermute(mine[0], "core", swap),)
    theirs = theirs + (lax.ppermute(mine[1], "core", swap),)
    weights = mine + theirs
    low = jnp.concatenate([line, before], axis=0)
    low_before = shift(low, False, 1)
    low_after = shift(low, False, -1)
    half = line.shape[0] // 2
    far = [shift(before[:half], True, 1), shift(after[half:], True, -1)]
    high = jnp.concatenate([after] + far, axis=0)
    high_after = shift(high, False, -1)
    high_before = shift(high, False, 1)
    low_far = shift(low_before, False, 1)
    high_far = shift(high_after, False, -1)

    named_by = jnp.any(
        expert_ids[:, :, None, None] == expert_ids[None, None, :, :], axis=3
    ).astype(jnp.int32)
    is_hot = jnp.sum(named_by, axis=2) > SLOTS
    tok_at = jnp.arange(tok_rows, dtype=jnp.int32)
    is_before = (tok_at[None, None, :] < tok_at[:, None, None]).astype(jnp.int32)
    slots = jnp.sum(named_by * is_before, axis=2)
    hot_id = jnp.max(jnp.where(is_hot, expert_ids, -1))
    cold_rows = columns * SLOTS
    rows = cold_rows + tok_rows
    place = expert_ids % columns // cores * (cores * SLOTS)
    place = place + jnp.bitwise_xor(expert_ids % cores, at_core) * SLOTS + slots
    place = jnp.where(is_hot, cold_rows + tok_at[:, None], place)
    place = (place + expert_ids // columns * rows).reshape(tok_rows * top_count, 1)

    lane_at = jnp.arange(2 * RING * RING, dtype=jnp.int32)
    offset_of = lambda at: jnp.where(at == 3, 2, jnp.where(at == 2, 1, -at))
    first = offset_of(lane_at % RING)
    second = offset_of(lane_at // RING % RING)
    y_to = (at_y + jnp.where(at_core == 0, first, second)) % groups
    x_to = (at_x + jnp.where(at_core == 0, second, first)) % width
    served_id = jnp.where(lane_at % CORES == 0, own, partner)
    flag = jnp.where(lane_at % RING < CORES, served_id, (served_id == hot_id).astype(jnp.int32))
    scalars = jnp.where(lane_at < RING * RING, x_to * groups + y_to, flag)

    served = None
    pieces = ((low, high), (low_before, high_before), (low_after, high_after), (low_far, high_far))
    for number, piece in enumerate(pieces):
        served = serve(scalars, number, *piece, weights, served, tok_rows, depth)

    lanes = served.shape[2]
    homes = groups * depth
    near = lax.all_to_all(
        served.reshape(width, homes, lanes), "x", split_axis=0, concat_axis=0, tiled=True
    )
    send = pl.pallas_call(
        functools.partial(assemble_kernel, tok_rows=tok_rows),
        in_specs=[
            pl.BlockSpec(memory_space=pltpu.SMEM),
            pl.BlockSpec(memory_space=pltpu.VMEM),
        ],
        out_shape=jax.ShapeDtypeStruct((homes * rows, quarter), BF16),
        scratch_shapes=[pltpu.VMEM((quarter // LANES, homes * rows, LANES), F32)],
        compiler_params=pltpu.CompilerParams(vmem_limit_bytes=16 * 2**20),
        name="assemble",
    )((hot_id % columns // cores).reshape(1), near).reshape(homes, rows, quarter)
    back = lax.all_to_all(send, ("dp", "z"), split_axis=0, concat_axis=0, tiled=True)
    pairs = tok_rows * top_count
    out = pl.pallas_call(
        home_kernel,
        out_shape=jax.ShapeDtypeStruct((pairs, groups * quarter), BF16),
        compiler_params=pltpu.CompilerParams(vmem_limit_bytes=16 * 2**20),
        name="home",
    )(place, route_gates.reshape(pairs, 1), back.reshape(groups, depth * rows, quarter))
    return out.reshape(tok_rows, top_count, groups * quarter)


def solution(mesh):
    groups = mesh.shape["dp"]
    sizes = (groups, mesh.shape["ep"] // (RING * CORES), RING, CORES)
    fine = Mesh(mesh.devices.reshape(sizes), ALL_AXES)

    def body(*args):
        return per_device(*args, sizes=sizes)

    return jax.shard_map(
        body,
        mesh=fine,
        in_specs=(
            P(ALL_AXES, None),
            P(ALL_AXES, None),
            P(ALL_AXES, None),
            P(EP_AXES, None, "dp"),
            P(EP_AXES, None, "dp"),
        ),
        out_specs=P(ALL_AXES, None, None),
        check_vma=False,
    )
```

```python
import functools

import jax
import jax.numpy as jnp
from jax import lax
from jax.experimental import pallas as pl
from jax.experimental.pallas import tpu as pltpu
from jax.sharding import Mesh, PartitionSpec as P


EP_AXES = ("z", "x", "core")
ALL_AXES = ("dp",) + EP_AXES
SLOTS = 2
LANES = 128
CORES = 2
RING = 4
F32 = jnp.float32
BF16 = jnp.bfloat16


def expert_kernel(
    scalar_ref, *refs, part_count, places, tok_rows, aliased
):
    parts, refs = refs[:part_count], refs[part_count:]
    gate0, up0, gate1, up1, *refs = refs
    out_ref, hidden_ref, ids_ref, pay_ref, sems = refs[1:] if aliased else refs
    width, quarter = gate0.shape
    block = sum(part.shape[0] for part in parts)
    homes = block // tok_rows
    rows = jnp.concatenate([part[:, :width] for part in parts], axis=0)
    at = 0
    for part in parts:
        ids_ref[at : at + part.shape[0], :] = part[:, width:].astype(F32)
        at += part.shape[0]
    for place, (gate, up) in enumerate(((gate0, up0), (gate1, up1))):
        gate_part = jnp.dot(rows, gate[...], preferred_element_type=F32)
        up_part = jnp.dot(rows, up[...], preferred_element_type=F32)
        hidden = (gate_part / (1.0 + jnp.exp(-gate_part)) * up_part).astype(BF16)
        for part in range(quarter // LANES):
            hidden_ref[place, part] = hidden[:, part * LANES : (part + 1) * LANES].astype(F32)

    def rows_at(place, tok):
        every = pl.ds(tok, homes, stride=tok_rows)
        parts = [hidden_ref[place, part, every, :] for part in range(quarter // LANES)]
        return jnp.concatenate(parts, axis=1)

    for place in range(CORES):
        expert = scalar_ref[RING * RING + place].astype(F32)
        count = jnp.zeros((homes, 1), F32)
        totals = [jnp.zeros((homes, quarter), F32) for _ in range(SLOTS)]
        for tok in range(tok_rows):
            every = pl.ds(tok, homes, stride=tok_rows)
            value = rows_at(place, tok)
            named = jnp.max(
                jnp.where(ids_ref[every, :] == expert, 1.0, 0.0), axis=1, keepdims=True
            )
            for slot in range(SLOTS):
                take = jnp.where(count == float(slot), named, 0.0)
                totals[slot] = totals[slot] + take * value
            count = count + named
        for slot in range(SLOTS):
            at = (place * SLOTS + slot) * quarter
            pay_ref[:, at : at + quarter] = totals[slot].astype(BF16)
    for tok in range(tok_rows):
        value = jnp.where(scalar_ref[RING * RING + CORES] > 0, rows_at(0, tok), 0.0)
        value += jnp.where(scalar_ref[RING * RING + CORES + 1] > 0, rows_at(1, tok), 0.0)
        at = (CORES * SLOTS + tok) * quarter
        pay_ref[:, at : at + quarter] = value.astype(BF16)

    depth = out_ref.shape[1]
    copies = [
        pltpu.make_async_copy(
            pay_ref.at[pl.ds(line * depth, depth)],
            out_ref.at[scalar_ref[place]],
            sems.at[line],
        )
        for line, place in enumerate(places)
    ]
    for copy in copies:
        copy.start()
    for copy in copies:
        copy.wait()


def serve(scalars, places, piece, weights, so_far, tok_rows, depth):
    quarter = weights[0].shape[1]
    block = sum(part.shape[0] for part in piece)
    lanes = (CORES * SLOTS + tok_rows) * quarter
    operands = [*piece, *weights]
    in_specs = [pl.BlockSpec(memory_space=pltpu.SMEM)]
    in_specs += [pl.BlockSpec(memory_space=pltpu.VMEM) for _ in operands]
    aliases = {}
    if so_far is not None:
        aliases = {1 + len(operands): 0}
        operands.append(so_far)
        in_specs.append(pl.BlockSpec(memory_space=pl.ANY))
    return pl.pallas_call(
        functools.partial(
            expert_kernel,
            part_count=len(piece),
            places=places,
            tok_rows=tok_rows,
            aliased=so_far is not None,
        ),
        in_specs=in_specs,
        out_specs=pl.BlockSpec(memory_space=pl.ANY),
        scratch_shapes=[
            pltpu.VMEM((CORES, quarter // LANES, block, LANES), F32),
            pltpu.VMEM((block, LANES), F32),
            pltpu.VMEM((block // tok_rows, lanes), BF16),
            pltpu.SemaphoreType.DMA((len(places),)),
        ],
        out_shape=jax.ShapeDtypeStruct((RING * RING, depth, lanes), BF16),
        input_output_aliases=aliases,
        compiler_params=pltpu.CompilerParams(vmem_limit_bytes=16 * 2**20),
        cost_estimate=pl.CostEstimate(
            flops=2 * block * weights[0].shape[0] * quarter * 4,
            bytes_accessed=2 * (block * piece[0].shape[1] + 4 * weights[0].size + len(places) * depth * lanes),
            transcendentals=2 * block * quarter,
        ),
        name="expert",
    )(scalars, *operands)


def assemble_kernel(hot_x_ref, near_ref, out_ref, wide_ref, *, tok_rows):
    _, homes, _ = near_ref.shape
    count = out_ref.shape[0] // homes
    quarter = out_ref.shape[1]
    parts = quarter // LANES
    for row in range(count):
        if row < count - tok_rows:
            source, entry = divmod(row, CORES * SLOTS)
        else:
            source, entry = hot_x_ref[0], row - (count - tok_rows) + CORES * SLOTS
        for part in range(parts):
            at = entry * quarter + part * LANES
            wide_ref[part, pl.ds(row, homes, stride=count), :] = near_ref[
                source, :, at : at + LANES
            ].astype(F32)
    for part in range(parts):
        out_ref[:, part * LANES : (part + 1) * LANES] = wide_ref[part].astype(BF16)


def home_kernel(place_ref, gate_ref, rows_ref, out_ref):
    pairs = out_ref.shape[0]
    groups, count, quarter = rows_ref.shape
    row_at = lax.broadcasted_iota(jnp.int32, (pairs, count), 1)
    pick = jnp.where(place_ref[...] == row_at, 1.0, 0.0).astype(BF16)
    gates = gate_ref[...]
    for group in range(groups):
        value = jnp.dot(pick, rows_ref[group], preferred_element_type=F32)
        out_ref[:, group * quarter : (group + 1) * quarter] = (gates * value).astype(BF16)


def per_device(tokens, expert_ids, route_gates, w_gate, w_up, *, sizes):
    tok_rows, top_count = expert_ids.shape
    model_width = tokens.shape[1]
    quarter = w_gate.shape[2]
    groups, depth, width, cores = sizes
    columns = width * cores
    at_y, at_z, at_x, at_core = (lax.axis_index(a).astype(jnp.int32) for a in ALL_AXES)
    own = (at_z * width + at_x) * cores + at_core
    partner = own + 1 - 2 * at_core

    def linear(y, z, x, core):
        return ((y % groups * depth + z) * width + x % width) * cores + core

    def shift(value, first, by):
        pairs = []
        for y in range(groups):
            for z in range(depth):
                for x in range(width):
                    for core in range(cores):
                        along_y = (core == 0) == first
                        to = (y + by, z, x, core) if along_y else (y, z, x + by, core)
                        pairs.append((linear(y, z, x, core), linear(*to)))
        return lax.ppermute(value, ALL_AXES, pairs)

    id_part = jnp.pad(
        expert_ids.astype(BF16), ((0, 0), (0, LANES - top_count)), constant_values=-1
    )
    line = lax.all_gather(
        jnp.concatenate([tokens, id_part], axis=1), "z", axis=0, tiled=True
    )
    expert_ids, w_gate, w_up, line = lax.optimization_barrier((expert_ids, w_gate, w_up, line))

    before = shift(line, True, 1)
    after = shift(line, True, -1)
    line_before = shift(line, False, 1)
    line_after = shift(line, False, -1)
    mine = (w_gate.reshape(model_width, quarter), w_up.reshape(model_width, quarter))
    swap = [(0, 1), (1, 0)]
    theirs = (lax.ppermute(mine[0], "core", swap),)
    theirs = theirs + (lax.ppermute(mine[1], "core", swap),)
    weights = mine + theirs
    mid = jnp.concatenate([before, after], axis=0)
    mid_before = shift(mid, False, 1)
    mid_after = shift(mid, False, -1)
    half = line.shape[0] // 2
    tail = [shift(before[:half], True, 1), shift(after[half:], True, -1)]
    line_far = shift(line_before, False, 1)
    tail = jnp.concatenate(tail, axis=0)
    tail_before = shift(tail, False, 1)
    tail_after = shift(tail, False, -1)
    mid_far = shift(mid_after, False, -1)
    tail_far = shift(tail_before, False, 1)

    named_by = jnp.any(
        expert_ids[:, :, None, None] == expert_ids[None, None, :, :], axis=3
    ).astype(jnp.int32)
    is_hot = jnp.sum(named_by, axis=2) > SLOTS
    tok_at = jnp.arange(tok_rows, dtype=jnp.int32)
    is_before = (tok_at[None, None, :] < tok_at[:, None, None]).astype(jnp.int32)
    slots = jnp.sum(named_by * is_before, axis=2)
    hot_id = jnp.max(jnp.where(is_hot, expert_ids, -1))
    cold_rows = columns * SLOTS
    rows = cold_rows + tok_rows
    place = expert_ids % columns // cores * (cores * SLOTS)
    place = place + jnp.bitwise_xor(expert_ids % cores, at_core) * SLOTS + slots
    place = jnp.where(is_hot, cold_rows + tok_at[:, None], place)
    place = (place + expert_ids // columns * rows).reshape(tok_rows * top_count, 1)

    lane_at = jnp.arange(2 * RING * RING, dtype=jnp.int32)
    offset_of = lambda at: jnp.where(at == 3, 2, jnp.where(at == 2, 1, -at))
    first = offset_of(lane_at % RING)
    second = offset_of(lane_at // RING % RING)
    y_to = (at_y + jnp.where(at_core == 0, first, second)) % groups
    x_to = (at_x + jnp.where(at_core == 0, second, first)) % width
    served_id = jnp.where(lane_at % CORES == 0, own, partner)
    flag = jnp.where(lane_at % RING < CORES, served_id, (served_id == hot_id).astype(jnp.int32))
    scalars = jnp.where(lane_at < RING * RING, x_to * groups + y_to, flag)

    served = None
    calls = (
        (("line", 0), ("mid", 0)),
        (("tail", 0), ("line", 1), ("mid", 1)),
        (("tail", 1), ("line", 2), ("mid", 2)),
        (("tail", 2), ("line", 3)),
        (("tail", 3), ("mid", 3)),
    )
    lines_of = {"line": (0,), "mid": (1, 2), "tail": (3,)}
    parts = {
        "line": (line, line_before, line_after, line_far),
        "mid": (mid, mid_before, mid_after, mid_far),
        "tail": (tail, tail_before, tail_after, tail_far),
    }
    for call in calls:
        places = tuple(RING * piece + j for kind, piece in call for j in lines_of[kind])
        piece_rows = tuple(parts[kind][piece] for kind, piece in call)
        served = serve(scalars, places, piece_rows, weights, served, tok_rows, depth)

    lanes = served.shape[2]
    homes = groups * depth
    near = lax.all_to_all(
        served.reshape(width, homes, lanes), "x", split_axis=0, concat_axis=0, tiled=True
    )
    send = pl.pallas_call(
        functools.partial(assemble_kernel, tok_rows=tok_rows),
        in_specs=[
            pl.BlockSpec(memory_space=pltpu.SMEM),
            pl.BlockSpec(memory_space=pltpu.VMEM),
        ],
        out_shape=jax.ShapeDtypeStruct((homes * rows, quarter), BF16),
        scratch_shapes=[pltpu.VMEM((quarter // LANES, homes * rows, LANES), F32)],
        compiler_params=pltpu.CompilerParams(vmem_limit_bytes=16 * 2**20),
        name="assemble",
    )((hot_id % columns // cores).reshape(1), near).reshape(homes, rows, quarter)
    back = lax.all_to_all(send, ("dp", "z"), split_axis=0, concat_axis=0, tiled=True)
    pairs = tok_rows * top_count
    out = pl.pallas_call(
        home_kernel,
        out_shape=jax.ShapeDtypeStruct((pairs, groups * quarter), BF16),
        compiler_params=pltpu.CompilerParams(vmem_limit_bytes=16 * 2**20),
        name="home",
    )(place, route_gates.reshape(pairs, 1), back.reshape(groups, depth * rows, quarter))
    return out.reshape(tok_rows, top_count, groups * quarter)


def solution(mesh):
    groups = mesh.shape["dp"]
    sizes = (groups, mesh.shape["ep"] // (RING * CORES), RING, CORES)
    fine = Mesh(mesh.devices.reshape(sizes), ALL_AXES)

    def body(*args):
        return per_device(*args, sizes=sizes)

    return jax.shard_map(
        body,
        mesh=fine,
        in_specs=(
            P(ALL_AXES, None),
            P(ALL_AXES, None),
            P(ALL_AXES, None),
            P(EP_AXES, None, "dp"),
            P(EP_AXES, None, "dp"),
        ),
        out_specs=P(ALL_AXES, None, None),
        check_vma=False,
    )
```

```python
import functools

import jax
import jax.numpy as jnp
from jax import lax
from jax.experimental import pallas as pl
from jax.experimental.pallas import tpu as pltpu
from jax.sharding import Mesh, PartitionSpec as P


EP_AXES = ("z", "x", "core")
ALL_AXES = ("dp",) + EP_AXES
SLOTS = 2
LANES = 128
CORES = 2
RING = 4
F32 = jnp.float32
BF16 = jnp.bfloat16


def expert_kernel(
    scalar_ref, *refs, part_count, places, tok_rows, aliased
):
    parts, refs = refs[:part_count], refs[part_count:]
    gate0, up0, gate1, up1, *refs = refs
    out_ref, hidden_ref, ids_ref, pay_ref, sems = refs[1:] if aliased else refs
    width, quarter = gate0.shape
    block = sum(part.shape[0] for part in parts)
    homes = block // tok_rows
    rows = jnp.concatenate([part[:, :width] for part in parts], axis=0)
    at = 0
    for part in parts:
        ids_ref[at : at + part.shape[0], :] = part[:, width:].astype(F32)
        at += part.shape[0]
    for place, (gate, up) in enumerate(((gate0, up0), (gate1, up1))):
        gate_part = jnp.dot(rows, gate[...], preferred_element_type=F32)
        up_part = jnp.dot(rows, up[...], preferred_element_type=F32)
        hidden = (gate_part / (1.0 + jnp.exp(-gate_part)) * up_part).astype(BF16)
        for part in range(quarter // LANES):
            hidden_ref[place, part] = hidden[:, part * LANES : (part + 1) * LANES].astype(F32)

    def rows_at(place, tok):
        every = pl.ds(tok, homes, stride=tok_rows)
        parts = [hidden_ref[place, part, every, :] for part in range(quarter // LANES)]
        return jnp.concatenate(parts, axis=1)

    for place in range(CORES):
        expert = scalar_ref[RING * RING + place].astype(F32)
        count = jnp.zeros((homes, 1), F32)
        totals = [jnp.zeros((homes, quarter), F32) for _ in range(SLOTS)]
        for tok in range(tok_rows):
            every = pl.ds(tok, homes, stride=tok_rows)
            value = rows_at(place, tok)
            named = jnp.max(
                jnp.where(ids_ref[every, :] == expert, 1.0, 0.0), axis=1, keepdims=True
            )
            for slot in range(SLOTS):
                take = jnp.where(count == float(slot), named, 0.0)
                totals[slot] = totals[slot] + take * value
            count = count + named
        for slot in range(SLOTS):
            at = (place * SLOTS + slot) * quarter
            pay_ref[:, at : at + quarter] = totals[slot].astype(BF16)
    for tok in range(tok_rows):
        value = jnp.where(scalar_ref[RING * RING + CORES] > 0, rows_at(0, tok), 0.0)
        value += jnp.where(scalar_ref[RING * RING + CORES + 1] > 0, rows_at(1, tok), 0.0)
        at = (CORES * SLOTS + tok) * quarter
        pay_ref[:, at : at + quarter] = value.astype(BF16)

    depth = out_ref.shape[1]
    copies = [
        pltpu.make_async_copy(
            pay_ref.at[pl.ds(line * depth, depth)],
            out_ref.at[scalar_ref[place]],
            sems.at[line],
        )
        for line, place in enumerate(places)
    ]
    for copy in copies:
        copy.start()
    for copy in copies:
        copy.wait()


def serve(scalars, places, piece, weights, so_far, tok_rows, depth):
    quarter = weights[0].shape[1]
    block = sum(part.shape[0] for part in piece)
    lanes = (CORES * SLOTS + tok_rows) * quarter
    operands = [*piece, *weights]
    in_specs = [pl.BlockSpec(memory_space=pltpu.SMEM)]
    in_specs += [pl.BlockSpec(memory_space=pltpu.VMEM) for _ in operands]
    aliases = {}
    if so_far is not None:
        aliases = {1 + len(operands): 0}
        operands.append(so_far)
        in_specs.append(pl.BlockSpec(memory_space=pl.ANY))
    return pl.pallas_call(
        functools.partial(
            expert_kernel,
            part_count=len(piece),
            places=places,
            tok_rows=tok_rows,
            aliased=so_far is not None,
        ),
        in_specs=in_specs,
        out_specs=pl.BlockSpec(memory_space=pl.ANY),
        scratch_shapes=[
            pltpu.VMEM((CORES, quarter // LANES, block, LANES), F32),
            pltpu.VMEM((block, LANES), F32),
            pltpu.VMEM((block // tok_rows, lanes), BF16),
            pltpu.SemaphoreType.DMA((len(places),)),
        ],
        out_shape=jax.ShapeDtypeStruct((RING * RING, depth, lanes), BF16),
        input_output_aliases=aliases,
        compiler_params=pltpu.CompilerParams(vmem_limit_bytes=16 * 2**20),
        cost_estimate=pl.CostEstimate(
            flops=2 * block * weights[0].shape[0] * quarter * 4,
            bytes_accessed=2 * (block * piece[0].shape[1] + 4 * weights[0].size + len(places) * depth * lanes),
            transcendentals=2 * block * quarter,
        ),
        name="expert",
    )(scalars, *operands)


def assemble_kernel(hot_x_ref, near_ref, out_ref, wide_ref, *, tok_rows):
    _, homes, _ = near_ref.shape
    count = out_ref.shape[0] // homes
    quarter = out_ref.shape[1]
    parts = quarter // LANES
    for row in range(count):
        if row < count - tok_rows:
            source, entry = divmod(row, CORES * SLOTS)
        else:
            source, entry = hot_x_ref[0], row - (count - tok_rows) + CORES * SLOTS
        for part in range(parts):
            at = entry * quarter + part * LANES
            wide_ref[part, pl.ds(row, homes, stride=count), :] = near_ref[
                source, :, at : at + LANES
            ].astype(F32)
    for part in range(parts):
        out_ref[:, part * LANES : (part + 1) * LANES] = wide_ref[part].astype(BF16)


def home_kernel(place_ref, gate_ref, rows_ref, out_ref):
    pairs = out_ref.shape[0]
    groups, count, quarter = rows_ref.shape
    row_at = lax.broadcasted_iota(jnp.int32, (pairs, count), 1)
    pick = jnp.where(place_ref[...] == row_at, 1.0, 0.0).astype(BF16)
    gates = gate_ref[...]
    for group in range(groups):
        value = jnp.dot(pick, rows_ref[group], preferred_element_type=F32)
        out_ref[:, group * quarter : (group + 1) * quarter] = (gates * value).astype(BF16)


def per_device(tokens, expert_ids, route_gates, w_gate, w_up, *, sizes):
    tok_rows, top_count = expert_ids.shape
    model_width = tokens.shape[1]
    quarter = w_gate.shape[2]
    groups, depth, width, cores = sizes
    columns = width * cores
    at_y, at_z, at_x, at_core = (lax.axis_index(a).astype(jnp.int32) for a in ALL_AXES)
    own = (at_z * width + at_x) * cores + at_core
    partner = own + 1 - 2 * at_core

    def linear(y, z, x, core):
        return ((y % groups * depth + z) * width + x % width) * cores + core

    def shift(value, first, by):
        pairs = []
        for y in range(groups):
            for z in range(depth):
                for x in range(width):
                    for core in range(cores):
                        along_y = (core == 0) == first
                        to = (y + by, z, x, core) if along_y else (y, z, x + by, core)
                        pairs.append((linear(y, z, x, core), linear(*to)))
        return lax.ppermute(value, ALL_AXES, pairs)

    id_part = jnp.pad(
        expert_ids.astype(BF16), ((0, 0), (0, LANES - top_count)), constant_values=-1
    )
    line = lax.all_gather(
        jnp.concatenate([tokens, id_part], axis=1), "z", axis=0, tiled=True
    )
    expert_ids, w_gate, w_up, line = lax.optimization_barrier((expert_ids, w_gate, w_up, line))

    before = shift(line, True, 1)
    after = shift(line, True, -1)
    line_before = shift(line, False, 1)
    line_after = shift(line, False, -1)
    mine = (w_gate.reshape(model_width, quarter), w_up.reshape(model_width, quarter))
    swap = [(0, 1), (1, 0)]
    theirs = (lax.ppermute(mine[0], "core", swap),)
    theirs = theirs + (lax.ppermute(mine[1], "core", swap),)
    weights = mine + theirs
    mid = jnp.concatenate([before, after], axis=0)
    mid_before = shift(mid, False, 1)
    mid_after = shift(mid, False, -1)
    half = line.shape[0] // 2
    tail = [shift(before[:half], True, 1), shift(after[half:], True, -1)]
    line_far = shift(line_after, False, -1)
    tail = jnp.concatenate(tail, axis=0)
    tail_before = shift(tail, False, 1)
    tail_after = shift(tail, False, -1)
    count = line.shape[0]
    low_far = shift(mid_before[:count], False, 1)
    high_far = shift(mid_after[count:], False, -1)
    tail_far = shift(tail_before, False, 1)

    named_by = jnp.any(
        expert_ids[:, :, None, None] == expert_ids[None, None, :, :], axis=3
    ).astype(jnp.int32)
    is_hot = jnp.sum(named_by, axis=2) > SLOTS
    tok_at = jnp.arange(tok_rows, dtype=jnp.int32)
    is_before = (tok_at[None, None, :] < tok_at[:, None, None]).astype(jnp.int32)
    slots = jnp.sum(named_by * is_before, axis=2)
    hot_id = jnp.max(jnp.where(is_hot, expert_ids, -1))
    cold_rows = columns * SLOTS
    rows = cold_rows + tok_rows
    place = expert_ids % columns // cores * (cores * SLOTS)
    place = place + jnp.bitwise_xor(expert_ids % cores, at_core) * SLOTS + slots
    place = jnp.where(is_hot, cold_rows + tok_at[:, None], place)
    place = (place + expert_ids // columns * rows).reshape(tok_rows * top_count, 1)

    lane_at = jnp.arange(2 * RING * RING, dtype=jnp.int32)
    offset_of = lambda at: jnp.where(at == 3, 2, jnp.where(at == 2, 1, -at))
    first = offset_of(lane_at % RING)
    second = offset_of(lane_at // RING % RING)
    y_to = (at_y + jnp.where(at_core == 0, first, second)) % groups
    x_to = (at_x + jnp.where(at_core == 0, second, first)) % width
    served_id = jnp.where(lane_at % CORES == 0, own, partner)
    flag = jnp.where(lane_at % RING < CORES, served_id, (served_id == hot_id).astype(jnp.int32))
    scalars = jnp.where(lane_at < RING * RING, x_to * groups + y_to, flag)

    served = None
    calls = (
        (("line", 0), ("mid", 0)),
        (("tail", 0), ("line", 1), ("mid", 1)),
        (("tail", 1), ("line", 2), ("mid", 2)),
        (("tail", 2), ("line", 3), ("low", 3), ("high", 3)),
        (("tail", 3),),
    )
    lines_of = {"line": (0,), "mid": (1, 2), "low": (1,), "high": (2,), "tail": (3,)}
    parts = {
        "line": (line, line_before, line_after, line_far),
        "mid": (mid, mid_before, mid_after),
        "low": (None, None, None, low_far),
        "high": (None, None, None, high_far),
        "tail": (tail, tail_before, tail_after, tail_far),
    }
    for call in calls:
        places = tuple(RING * piece + j for kind, piece in call for j in lines_of[kind])
        piece_rows = tuple(parts[kind][piece] for kind, piece in call)
        served = serve(scalars, places, piece_rows, weights, served, tok_rows, depth)

    lanes = served.shape[2]
    homes = groups * depth
    near = lax.all_to_all(
        served.reshape(width, homes, lanes), "x", split_axis=0, concat_axis=0, tiled=True
    )
    send = pl.pallas_call(
        functools.partial(assemble_kernel, tok_rows=tok_rows),
        in_specs=[
            pl.BlockSpec(memory_space=pltpu.SMEM),
            pl.BlockSpec(memory_space=pltpu.VMEM),
        ],
        out_shape=jax.ShapeDtypeStruct((homes * rows, quarter), BF16),
        scratch_shapes=[pltpu.VMEM((quarter // LANES, homes * rows, LANES), F32)],
        compiler_params=pltpu.CompilerParams(vmem_limit_bytes=16 * 2**20),
        name="assemble",
    )((hot_id % columns // cores).reshape(1), near).reshape(homes, rows, quarter)
    back = lax.all_to_all(send, ("dp", "z"), split_axis=0, concat_axis=0, tiled=True)
    pairs = tok_rows * top_count
    out = pl.pallas_call(
        home_kernel,
        out_shape=jax.ShapeDtypeStruct((pairs, groups * quarter), BF16),
        compiler_params=pltpu.CompilerParams(vmem_limit_bytes=16 * 2**20),
        name="home",
    )(place, route_gates.reshape(pairs, 1), back.reshape(groups, depth * rows, quarter))
    return out.reshape(tok_rows, top_count, groups * quarter)


def solution(mesh):
    groups = mesh.shape["dp"]
    sizes = (groups, mesh.shape["ep"] // (RING * CORES), RING, CORES)
    fine = Mesh(mesh.devices.reshape(sizes), ALL_AXES)

    def body(*args):
        return per_device(*args, sizes=sizes)

    return jax.shard_map(
        body,
        mesh=fine,
        in_specs=(
            P(ALL_AXES, None),
            P(ALL_AXES, None),
            P(ALL_AXES, None),
            P(EP_AXES, None, "dp"),
            P(EP_AXES, None, "dp"),
        ),
        out_specs=P(ALL_AXES, None, None),
        check_vma=False,
    )
```

```python
import functools

import jax
import jax.numpy as jnp
from jax import lax
from jax.experimental import pallas as pl
from jax.experimental.pallas import tpu as pltpu
from jax.sharding import Mesh, PartitionSpec as P


EP_AXES = ("z", "x", "core")
ALL_AXES = ("dp",) + EP_AXES
SLOTS = 2
LANES = 128
CORES = 2
RING = 4
F32 = jnp.float32
BF16 = jnp.bfloat16


def expert_kernel(
    scalar_ref, line_ref, mid_ref, tail_ref, *rest, number, tok_rows, aliased
):
    gate0, up0, gate1, up1, *refs = rest
    out_ref, hidden_ref, ids_ref, pay_ref, sems = refs[1:] if aliased else refs
    width, quarter = gate0.shape
    parts = (line_ref, mid_ref, tail_ref)
    block = sum(part.shape[0] for part in parts)
    homes = block // tok_rows
    rows = jnp.concatenate([part[:, :width] for part in parts], axis=0)
    at = 0
    for part in parts:
        ids_ref[at : at + part.shape[0], :] = part[:, width:].astype(F32)
        at += part.shape[0]
    for place, (gate, up) in enumerate(((gate0, up0), (gate1, up1))):
        gate_part = jnp.dot(rows, gate[...], preferred_element_type=F32)
        up_part = jnp.dot(rows, up[...], preferred_element_type=F32)
        hidden = (gate_part / (1.0 + jnp.exp(-gate_part)) * up_part).astype(BF16)
        for part in range(quarter // LANES):
            hidden_ref[place, part] = hidden[:, part * LANES : (part + 1) * LANES].astype(F32)

    def rows_at(place, tok):
        every = pl.ds(tok, homes, stride=tok_rows)
        parts = [hidden_ref[place, part, every, :] for part in range(quarter // LANES)]
        return jnp.concatenate(parts, axis=1)

    for place in range(CORES):
        expert = scalar_ref[RING * RING + place].astype(F32)
        count = jnp.zeros((homes, 1), F32)
        totals = [jnp.zeros((homes, quarter), F32) for _ in range(SLOTS)]
        for tok in range(tok_rows):
            every = pl.ds(tok, homes, stride=tok_rows)
            value = rows_at(place, tok)
            named = jnp.max(
                jnp.where(ids_ref[every, :] == expert, 1.0, 0.0), axis=1, keepdims=True
            )
            for slot in range(SLOTS):
                take = jnp.where(count == float(slot), named, 0.0)
                totals[slot] = totals[slot] + take * value
            count = count + named
        for slot in range(SLOTS):
            at = (place * SLOTS + slot) * quarter
            pay_ref[:, at : at + quarter] = totals[slot].astype(BF16)
    for tok in range(tok_rows):
        value = jnp.where(scalar_ref[RING * RING + CORES] > 0, rows_at(0, tok), 0.0)
        value += jnp.where(scalar_ref[RING * RING + CORES + 1] > 0, rows_at(1, tok), 0.0)
        at = (CORES * SLOTS + tok) * quarter
        pay_ref[:, at : at + quarter] = value.astype(BF16)

    depth = out_ref.shape[1]
    copies = [
        pltpu.make_async_copy(
            pay_ref.at[pl.ds(line * depth, depth)],
            out_ref.at[scalar_ref[RING * number + line]],
            sems.at[line],
        )
        for line in range(RING)
    ]
    for copy in copies:
        copy.start()
    for copy in copies:
        copy.wait()


def serve(scalars, number, piece, weights, so_far, tok_rows, depth):
    quarter = weights[0].shape[1]
    block = sum(part.shape[0] for part in piece)
    lanes = (CORES * SLOTS + tok_rows) * quarter
    operands = [*piece, *weights]
    in_specs = [pl.BlockSpec(memory_space=pltpu.SMEM)]
    in_specs += [pl.BlockSpec(memory_space=pltpu.VMEM) for _ in operands]
    aliases = {}
    if so_far is not None:
        aliases = {1 + len(operands): 0}
        operands.append(so_far)
        in_specs.append(pl.BlockSpec(memory_space=pl.ANY))
    return pl.pallas_call(
        functools.partial(
            expert_kernel, number=number, tok_rows=tok_rows, aliased=so_far is not None
        ),
        in_specs=in_specs,
        out_specs=pl.BlockSpec(memory_space=pl.ANY),
        scratch_shapes=[
            pltpu.VMEM((CORES, quarter // LANES, block, LANES), F32),
            pltpu.VMEM((block, LANES), F32),
            pltpu.VMEM((block // tok_rows, lanes), BF16),
            pltpu.SemaphoreType.DMA((RING,)),
        ],
        out_shape=jax.ShapeDtypeStruct((RING * RING, depth, lanes), BF16),
        input_output_aliases=aliases,
        compiler_params=pltpu.CompilerParams(vmem_limit_bytes=16 * 2**20),
        cost_estimate=pl.CostEstimate(
            flops=2 * block * weights[0].shape[0] * quarter * 4,
            bytes_accessed=2 * (block * piece[0].shape[1] + 4 * weights[0].size + RING * depth * lanes),
            transcendentals=2 * block * quarter,
        ),
        name="expert",
    )(scalars, *operands)


def assemble_kernel(hot_x_ref, near_ref, out_ref, wide_ref, *, tok_rows):
    _, homes, _ = near_ref.shape
    count = out_ref.shape[0] // homes
    quarter = out_ref.shape[1]
    parts = quarter // LANES
    for row in range(count):
        if row < count - tok_rows:
            source, entry = divmod(row, CORES * SLOTS)
        else:
            source, entry = hot_x_ref[0], row - (count - tok_rows) + CORES * SLOTS
        for part in range(parts):
            at = entry * quarter + part * LANES
            wide_ref[part, pl.ds(row, homes, stride=count), :] = near_ref[
                source, :, at : at + LANES
            ].astype(F32)
    for part in range(parts):
        out_ref[:, part * LANES : (part + 1) * LANES] = wide_ref[part].astype(BF16)


def home_kernel(place_ref, gate_ref, rows_ref, out_ref):
    pairs = out_ref.shape[0]
    groups, count, quarter = rows_ref.shape
    row_at = lax.broadcasted_iota(jnp.int32, (pairs, count), 1)
    pick = jnp.where(place_ref[...] == row_at, 1.0, 0.0).astype(BF16)
    gates = gate_ref[...]
    for group in range(groups):
        value = jnp.dot(pick, rows_ref[group], preferred_element_type=F32)
        out_ref[:, group * quarter : (group + 1) * quarter] = (gates * value).astype(BF16)


def per_device(tokens, expert_ids, route_gates, w_gate, w_up, *, sizes):
    tok_rows, top_count = expert_ids.shape
    model_width = tokens.shape[1]
    quarter = w_gate.shape[2]
    groups, depth, width, cores = sizes
    columns = width * cores
    at_y, at_z, at_x, at_core = (lax.axis_index(a).astype(jnp.int32) for a in ALL_AXES)
    own = (at_z * width + at_x) * cores + at_core
    partner = own + 1 - 2 * at_core

    def linear(y, z, x, core):
        return ((y % groups * depth + z) * width + x % width) * cores + core

    def shift(value, first, by):
        pairs = []
        for y in range(groups):
            for z in range(depth):
                for x in range(width):
                    for core in range(cores):
                        along_y = (core == 0) == first
                        to = (y + by, z, x, core) if along_y else (y, z, x + by, core)
                        pairs.append((linear(y, z, x, core), linear(*to)))
        return lax.ppermute(value, ALL_AXES, pairs)

    id_part = jnp.pad(
        expert_ids.astype(BF16), ((0, 0), (0, LANES - top_count)), constant_values=-1
    )
    line = lax.all_gather(
        jnp.concatenate([tokens, id_part], axis=1), "z", axis=0, tiled=True
    )
    expert_ids, w_gate, w_up, line = lax.optimization_barrier((expert_ids, w_gate, w_up, line))

    before = shift(line, True, 1)
    after = shift(line, True, -1)
    line_before = shift(line, False, 1)
    line_after = shift(line, False, -1)
    mine = (w_gate.reshape(model_width, quarter), w_up.reshape(model_width, quarter))
    swap = [(0, 1), (1, 0)]
    theirs = (lax.ppermute(mine[0], "core", swap),)
    theirs = theirs + (lax.ppermute(mine[1], "core", swap),)
    weights = mine + theirs
    mid = jnp.concatenate([before, after], axis=0)
    mid_before = shift(mid, False, 1)
    mid_after = shift(mid, False, -1)
    half = line.shape[0] // 2
    tail = [shift(before[:half], True, 1), shift(after[half:], True, -1)]
    line_far = shift(line_before, False, 1)
    tail = jnp.concatenate(tail, axis=0)
    tail_before = shift(tail, False, 1)
    tail_after = shift(tail, False, -1)
    mid_far = shift(mid_after, False, -1)
    tail_far = shift(tail_before, False, 1)

    named_by = jnp.any(
        expert_ids[:, :, None, None] == expert_ids[None, None, :, :], axis=3
    ).astype(jnp.int32)
    is_hot = jnp.sum(named_by, axis=2) > SLOTS
    tok_at = jnp.arange(tok_rows, dtype=jnp.int32)
    is_before = (tok_at[None, None, :] < tok_at[:, None, None]).astype(jnp.int32)
    slots = jnp.sum(named_by * is_before, axis=2)
    hot_id = jnp.max(jnp.where(is_hot, expert_ids, -1))
    cold_rows = columns * SLOTS
    rows = cold_rows + tok_rows
    place = expert_ids % columns // cores * (cores * SLOTS)
    place = place + jnp.bitwise_xor(expert_ids % cores, at_core) * SLOTS + slots
    place = jnp.where(is_hot, cold_rows + tok_at[:, None], place)
    place = (place + expert_ids // columns * rows).reshape(tok_rows * top_count, 1)

    lane_at = jnp.arange(2 * RING * RING, dtype=jnp.int32)
    offset_of = lambda at: jnp.where(at == 3, 2, jnp.where(at == 2, 1, -at))
    first = offset_of(lane_at % RING)
    second = offset_of(lane_at // RING % RING)
    y_to = (at_y + jnp.where(at_core == 0, first, second)) % groups
    x_to = (at_x + jnp.where(at_core == 0, second, first)) % width
    served_id = jnp.where(lane_at % CORES == 0, own, partner)
    flag = jnp.where(lane_at % RING < CORES, served_id, (served_id == hot_id).astype(jnp.int32))
    scalars = jnp.where(lane_at < RING * RING, x_to * groups + y_to, flag)

    served = None
    pieces = (
        (line, mid, tail),
        (line_before, mid_before, tail_before),
        (line_after, mid_after, tail_after),
        (line_far, mid_far, tail_far),
    )
    for number, piece in enumerate(pieces):
        served = serve(scalars, number, piece, weights, served, tok_rows, depth)

    lanes = served.shape[2]
    homes = groups * depth
    near = lax.all_to_all(
        served.reshape(width, homes, lanes), "x", split_axis=0, concat_axis=0, tiled=True
    )
    send = pl.pallas_call(
        functools.partial(assemble_kernel, tok_rows=tok_rows),
        in_specs=[
            pl.BlockSpec(memory_space=pltpu.SMEM),
            pl.BlockSpec(memory_space=pltpu.VMEM),
        ],
        out_shape=jax.ShapeDtypeStruct((homes * rows, quarter), BF16),
        scratch_shapes=[pltpu.VMEM((quarter // LANES, homes * rows, LANES), F32)],
        compiler_params=pltpu.CompilerParams(vmem_limit_bytes=16 * 2**20),
        name="assemble",
    )((hot_id % columns // cores).reshape(1), near).reshape(homes, rows, quarter)
    back = lax.all_to_all(send, ("dp", "z"), split_axis=0, concat_axis=0, tiled=True)
    pairs = tok_rows * top_count
    out = pl.pallas_call(
        home_kernel,
        out_shape=jax.ShapeDtypeStruct((pairs, groups * quarter), BF16),
        compiler_params=pltpu.CompilerParams(vmem_limit_bytes=16 * 2**20),
        name="home",
    )(place, route_gates.reshape(pairs, 1), back.reshape(groups, depth * rows, quarter))
    return out.reshape(tok_rows, top_count, groups * quarter)


def solution(mesh):
    groups = mesh.shape["dp"]
    sizes = (groups, mesh.shape["ep"] // (RING * CORES), RING, CORES)
    fine = Mesh(mesh.devices.reshape(sizes), ALL_AXES)

    def body(*args):
        return per_device(*args, sizes=sizes)

    return jax.shard_map(
        body,
        mesh=fine,
        in_specs=(
            P(ALL_AXES, None),
            P(ALL_AXES, None),
            P(ALL_AXES, None),
            P(EP_AXES, None, "dp"),
            P(EP_AXES, None, "dp"),
        ),
        out_specs=P(ALL_AXES, None, None),
        check_vma=False,
    )
```
